512 devices in a mesh: ctx: 64 (over y, z), tp: 8 (over x, core).
Axes of the slice: x: 4, y: 4, z: 16, core: 2. Of those that a mesh axis runs over, the one named last changes fastest.
Arguments:
- queries: bfloat16 [16384, 4096], P('ctx', 'tp'), may hold values from -112 to 112
- keys: bfloat16 [16384, 1024], P('ctx', 'tp'), may hold values from -4.5 to 4.5
- values: bfloat16 [16384, 1024], P('ctx', 'tp'), may hold values from -6 to 6
- head_kind: int32 [8], replicated, may hold values from 0 to 1, as said below
- sink_len: int32 [8], replicated, may hold values from 32 to 128, as said below
- window_len: int32 [8], replicated, may hold values from 512 to 1024, as said below
- w_out: bfloat16 [4096, 4096], P('tp'), may hold values from -0.375 to 0.375
Outputs:
- mixed: bfloat16 [16384, 4096], P(('ctx', 'tp'))
The draws below stay inside these ranges and needn't reach their ends.
Inputs may be any that keep to these rules, and one draw needn't show every extreme that they name: `head_kind`: exactly 4 entries are 1. `sink_len`: some head with head_kind 0 has exactly 128. `window_len`: some head with head_kind 0 has exactly 1024.
All inputs are finite; a program needn't handle non-finite values.
Results may differ from the reference program's by a relative error of at most 0.014.
Values may be sent and summed in bfloat16 or wider, within the bound.
No kernel may reach another device: no remote copies, remote signals or barrier semaphores. Data moves between devices by JAX's collectives and lax.ppermute only.
A program may use at most 64 MiB of HBM per device.

```python
import math
import jax
import jax.numpy as jnp
from jax import lax

H = 32
KVH = 8
HD = 128
D = 4096
GROUP = 4
TOKENS = 16384
SINK = 128
WINDOW = 1024


def query_key_pair(key):
    query_noise = jax.random.normal(jax.random.fold_in(key, 101), (TOKENS, KVH, GROUP, HD), jnp.float32)
    key_noise = jax.random.normal(jax.random.fold_in(key, 102), (TOKENS, KVH, HD), jnp.float32)
    query_draw = jnp.clip(2.0 * query_noise, -8.0, 8.0)
    key_draw = jnp.clip(key_noise, -4.0, 4.0)
    return (query_draw.reshape(TOKENS, H * HD), key_draw.reshape(TOKENS, KVH * HD))


def draw_queries(key, part):
    return query_key_pair(key)[0].astype(jnp.bfloat16)


def draw_keys(key, part):
    return query_key_pair(key)[1].astype(jnp.bfloat16)


def head_table(key):
    order = jax.random.permutation(jax.random.fold_in(key, 201), KVH)
    kinds = (order < KVH // 2).astype(jnp.int32)
    widest = order == KVH // 2
    sinks = jax.random.randint(jax.random.fold_in(key, 202), (KVH,), SINK // 4, SINK + 1)
    windows = jax.random.randint(jax.random.fold_in(key, 203), (KVH,), WINDOW // 2, WINDOW + 1)
    sinks = jnp.where(widest, SINK, sinks).astype(jnp.int32)
    windows = jnp.where(widest, WINDOW, windows).astype(jnp.int32)
    return (kinds, sinks, windows)


def draw_head_kind(key, part):
    return head_table(key)[0]


def draw_sink_len(key, part):
    return head_table(key)[1]


def draw_window_len(key, part):
    return head_table(key)[2]


def block_levels(rng, shape, shards, least, high):
    def one(dim, parts):
        heights = jax.random.uniform(jax.random.fold_in(jax.random.fold_in(rng, 6), dim), (parts,), jnp.float32, least / len(shards), high / len(shards))
        return jnp.repeat(jnp.exp(heights), shape[dim] // parts).reshape((-1,) + (1,) * (len(shape) - dim - 1))

    loudness = one(*shards[0])
    for cut in shards[1:]:
        loudness = loudness * one(*cut)
    return loudness


def centred(stream_key, extent, deviation, bound, split=(), kind=jnp.bfloat16):
    result = deviation * jax.random.normal(stream_key, extent, jnp.float32)
    if split:
        result = result * block_levels(stream_key, extent, split, -0.22, 0.18)
    return jnp.clip(result, -bound, bound).astype(kind)


def setup_inputs(seed: int = 0) -> dict:
    splits = jax.random.split(jax.random.key(seed), 8)
    return {
        "queries": draw_queries(jax.random.fold_in(splits[7], 71), 0),
        "keys": draw_keys(jax.random.fold_in(splits[7], 71), 0),
        "values": centred(splits[2], (TOKENS, KVH * HD), 1.0, 6.0, ((0, 64), (1, 8))),
        "head_kind": draw_head_kind(jax.random.fold_in(splits[7], 71), 0),
        "sink_len": draw_sink_len(jax.random.fold_in(splits[7], 71), 0),
        "window_len": draw_window_len(jax.random.fold_in(splits[7], 71), 0),
        "w_out": centred(splits[6], (H * HD, D), (H * HD // 16) ** -0.5, 0.375, ((0, 8),)),
    }


def reference(queries, keys, values, head_kind, sink_len, window_len, w_out):
    score_scale = 1.0 / math.sqrt(HD)
    q_all = queries.reshape(TOKENS, KVH, GROUP, HD)
    k_all = keys.reshape(TOKENS, KVH, HD)
    v_all = values.reshape(TOKENS, KVH, HD)
    positions = jnp.arange(TOKENS, dtype=jnp.int32)
    block_size = min(512, TOKENS)

    def head_output(kv_head):
        q_head = lax.dynamic_index_in_dim(q_all, kv_head, 1, keepdims=False).astype(jnp.float32)
        k_head = lax.dynamic_index_in_dim(k_all, kv_head, 1, keepdims=False).astype(jnp.float32)
        v_head = lax.dynamic_index_in_dim(v_all, kv_head, 1, keepdims=False).astype(jnp.float32)
        retrieval = head_kind[kv_head] == 1
        sink_count = sink_len[kv_head]
        window = window_len[kv_head]

        def block_output(block_index):
            q_block = lax.dynamic_slice_in_dim(q_head, block_index * block_size, block_size, 0)
            q_pos = block_index * block_size + jnp.arange(block_size, dtype=jnp.int32)
            scores = jnp.einsum('igd,jd->igj', q_block, k_head) * score_scale
            before = positions[None, :] <= q_pos[:, None]
            in_window = positions[None, :] > q_pos[:, None] - window
            in_sink = positions[None, :] < sink_count
            allowed = (before & (retrieval | in_window | in_sink))[:, None, :]
            top_score = lax.optimization_barrier(jnp.max(jnp.where(allowed, scores, -jnp.inf), axis=2, keepdims=True))
            weights = jnp.where(allowed, jnp.exp(scores - top_score), 0.0)
            weight_sum = lax.optimization_barrier(jnp.sum(weights, axis=2))
            rounded = lax.optimization_barrier(weights.astype(jnp.bfloat16)).astype(jnp.float32)
            blended = jnp.einsum('igj,jd->igd', rounded, v_head) / weight_sum[:, :, None]
            return blended.astype(jnp.bfloat16)
        blocks_out = lax.map(block_output, jnp.arange(TOKENS // block_size, dtype=jnp.int32))
        return blocks_out.reshape(TOKENS, GROUP * HD)
    per_head = lax.map(head_output, jnp.arange(KVH, dtype=jnp.int32))
    attention = jnp.transpose(per_head, (1, 0, 2)).reshape(TOKENS, KVH * GROUP * HD)
    return jnp.dot(attention, w_out, preferred_element_type=jnp.float32).astype(jnp.bfloat16)
```

```python
import functools
import math

import jax
import jax.numpy as jnp
from jax import lax
from jax.experimental import pallas as pl
from jax.experimental.pallas import tpu as pltpu
from jax.sharding import Mesh
from jax.sharding import PartitionSpec as P

HD = 128
GROUP = 4
NY, NZ, NX, NC = 4, 16, 4, 2
ROWS = 256
ROW_KEYS = NZ * ROWS
LOW = -1e30
MASKED = -3e30
SCALE = 1.0 / math.sqrt(HD)
EXP2_SCALE = SCALE * math.log2(math.e)
LN2 = math.log(2.0)
PACK = GROUP * HD + 128
NT = (((1,), (1,)), ((), ()))


def fold(q_ref, slot, blocks, masks, acc, top, total):
    for h in range(GROUP):
        q = q_ref[slot, :, h * HD : (h + 1) * HD]
        scores = []
        for block, mask in zip(blocks, masks):
            s = lax.dot_general(q, block[:, :HD], NT, preferred_element_type=jnp.float32)
            if mask is not None:
                s = jnp.where(mask, s, MASKED)
            scores.append(s)
        peak = functools.reduce(jnp.maximum, scores)
        old = top[slot, h]
        new = jnp.maximum(old, jnp.max(peak, axis=1, keepdims=True))
        factor = jnp.exp2((old - new) * EXP2_SCALE)
        shift = new[:, :1] * EXP2_SCALE
        out = None
        part = None
        for s, block in zip(scores, blocks):
            w = jnp.exp2(s * EXP2_SCALE - shift)
            lanes = w[:, :128] + w[:, 128:]
            part = lanes if part is None else part + lanes
            o = jnp.dot(
                w.astype(jnp.bfloat16), block[:, HD:], preferred_element_type=jnp.float32
            )
            out = o if out is None else out + o
        top[slot, h] = new
        total[slot, h] = total[slot, h] * factor + part
        acc[slot, h] = acc[slot, h] * factor + out


def fold_masked(info, q_ref, slot, block_ref, key_start, acc, top, total):
    kind, sink, window = info[2], info[3], info[4]
    query_start = (info[0] + slot) * ROW_KEYS + info[1] * ROWS
    needed = (key_start <= query_start + ROWS - 1) & (
        (kind == 1) | (key_start + ROWS - 1 > query_start - window) | (key_start < sink)
    )

    @pl.when(needed)
    def _():
        i = query_start + lax.broadcasted_iota(jnp.int32, (ROWS, ROWS), 0)
        j = key_start + lax.broadcasted_iota(jnp.int32, (ROWS, ROWS), 1)
        mask = (j <= i) & ((kind == 1) | (j > i - window) | (j < sink))
        fold(q_ref, slot, [block_ref[...]], [mask], acc, top, total)


def first_kernel(info, q_ref, own_ref, acc, top, total):
    acc[...] = jnp.zeros_like(acc)
    top[...] = jnp.full_like(top, LOW)
    total[...] = jnp.zeros_like(total)
    own_start = info[0] * ROW_KEYS + info[1] * ROWS
    fold_masked(info, q_ref, 0, own_ref, own_start, acc, top, total)


def step_kernel(
    distance, last, info, q0_ref, q1_ref, q2_ref, q3_ref, a_ref, b_ref,
    acc_in, top_in, total_in, acc, top, total, q_ref
):
    del acc_in, top_in, total_in
    y, z, kind = info[0], info[1], info[2]
    slots = NY - y
    a_start = y * ROW_KEYS + lax.rem(z - distance + NZ, NZ) * ROWS
    b_start = y * ROW_KEYS + lax.rem(z + (0 if last else distance), NZ) * ROWS
    q_ref[0] = q0_ref[...]
    q_ref[1] = q1_ref[...]
    q_ref[2] = q2_ref[...]
    q_ref[3] = q3_ref[...]

    fold_masked(info, q_ref, 0, a_ref, a_start, acc, top, total)
    if not last:
        fold_masked(info, q_ref, 0, b_ref, b_start, acc, top, total)

    @pl.when(kind == 1)
    def _():
        @pl.loop(1, slots)
        def _(slot):
            fold(q_ref, slot, [a_ref[...], b_ref[...]], [None, None], acc, top, total)

    @pl.when(kind != 1)
    def _():
        @pl.loop(1, slots)
        def _(slot):
            fold_masked(info, q_ref, slot, a_ref, a_start, acc, top, total)
            fold_masked(info, q_ref, slot, b_ref, b_start, acc, top, total)


def finish_kernel(info, acc, top, total, out_ref):
    y = info[0]
    lane = lax.broadcasted_iota(jnp.int32, (ROWS, 128), 1)
    for target in range(NY):
        slot = jnp.maximum(target - y, 0)
        valid = target >= y
        stats = jnp.full((ROWS, 128), LOW, jnp.float32)
        for h in range(GROUP):
            s = jnp.sum(total[slot, h], axis=1, keepdims=True)
            have = (s > 0.0) & valid
            safe = jnp.where(have, s, 1.0)
            o = jnp.where(have, acc[slot, h] / safe, 0.0).astype(jnp.bfloat16)
            lse = jnp.where(have, top[slot, h] * SCALE + jnp.log(safe), LOW)
            stats = jnp.where(lane // 32 == h, lse, stats)
            for x in range(NX):
                for c in range(NC):
                    r = (x * NC + c) * 32
                    out_ref[target * NC + c, x * 32 : x * 32 + 32, h * HD : (h + 1) * HD] = o[
                        r : r + 32
                    ]
        high = stats.astype(jnp.bfloat16).astype(jnp.float32)
        rest = stats - high
        mid = rest.astype(jnp.bfloat16).astype(jnp.float32)
        low = rest - mid
        which = lane % 32
        packed = jnp.where(
            which == 0, high, jnp.where(which == 1, mid, jnp.where(which == 2, low, 0.0))
        ).astype(jnp.bfloat16)
        for x in range(NX):
            for c in range(NC):
                r = (x * NC + c) * 32
                out_ref[target * NC + c, x * 32 : x * 32 + 32, GROUP * HD :] = packed[r : r + 32]


def project_kernel(info, parts_ref, own_w_ref, other_w_ref, out_ref, mix):
    @pl.when(pl.program_id(0) == 0)
    def _():
        core = info[5]
        lane = lax.broadcasted_iota(jnp.int32, (128, 128), 1)
        for place in range(NC):
            source = core if place == 0 else 1 - core
            stats = [parts_ref[y * NC + source, :, GROUP * HD :].astype(jnp.float32) for y in range(NY)]
            for h in range(GROUP):
                here = (lane // 32) == h
                lse = [
                    jnp.sum(jnp.where(here, s, 0.0), axis=1, keepdims=True) for s in stats
                ]
                peak = functools.reduce(jnp.maximum, lse)
                weight = [jnp.exp(v - peak) for v in lse]
                norm = functools.reduce(jnp.add, weight)
                out = None
                for y in range(NY):
                    o = parts_ref[y * NC + source, :, h * HD : (h + 1) * HD].astype(jnp.float32)
                    o = o * weight[y]
                    out = o if out is None else out + o
                mix[place, :, h * HD : (h + 1) * HD] = (out / norm).astype(jnp.bfloat16)

    out_ref[...] = (
        jnp.dot(mix[0], own_w_ref[...], preferred_element_type=jnp.float32)
        + jnp.dot(mix[1], other_w_ref[...], preferred_element_type=jnp.float32)
    ).astype(jnp.bfloat16)


VMEM_SPEC = pl.BlockSpec(memory_space=pltpu.VMEM)
SMEM_SPEC = pl.BlockSpec(memory_space=pltpu.SMEM)
STATE = [
    jax.ShapeDtypeStruct((NY, GROUP, ROWS, HD), jnp.float32),
    jax.ShapeDtypeStruct((NY, GROUP, ROWS, 128), jnp.float32),
    jax.ShapeDtypeStruct((NY, GROUP, ROWS, 128), jnp.float32),
]


def params(mib=24):
    return pltpu.CompilerParams(vmem_limit_bytes=mib << 20)


def body(queries, keys, values, head_kind, sink_len, window_len, w_out):
    y, z = lax.axis_index("y"), lax.axis_index("z")
    x, core = lax.axis_index("x"), lax.axis_index("core")
    head = x * NC + core
    info = jnp.stack([y, z, head_kind[head], sink_len[head], window_len[head], core]).astype(jnp.int32)
    own = jnp.concatenate([keys, values], axis=1)

    ahead = [(i, (i + 1) % NZ) for i in range(NZ)]
    behind = [(i, (i - 1) % NZ) for i in range(NZ)]
    a = lax.ppermute(own, "z", ahead)
    b = lax.ppermute(own, "z", behind)
    received = [
        lax.ppermute(queries, "y", [(i, i - d) for i in range(d, NY)]) for d in range(1, NY)
    ]
    other_w = lax.ppermute(w_out, "core", [(0, 1), (1, 0)])

    cost = pl.CostEstimate(flops=1 << 30, bytes_accessed=8 << 20, transcendentals=1 << 22)
    state = pl.pallas_call(
        first_kernel,
        out_shape=STATE,
        in_specs=[SMEM_SPEC, VMEM_SPEC, VMEM_SPEC],
        out_specs=[VMEM_SPEC] * 3,
        compiler_params=params(),
        cost_estimate=cost,
        name="first",
    )(info, queries[None], own)

    for distance in range(1, NZ // 2 + 1):
        last = distance == NZ // 2
        here_a, here_b = a, own if last else b
        if not last:
            a = lax.ppermute(a, "z", ahead)
            if distance + 1 < NZ // 2:
                b = lax.ppermute(b, "z", behind)
        state = pl.pallas_call(
            functools.partial(step_kernel, distance, last),
            out_shape=STATE,
            in_specs=[SMEM_SPEC] + [VMEM_SPEC] * 9,
            out_specs=[VMEM_SPEC] * 3,
            scratch_shapes=[pltpu.VMEM((NY, ROWS, GROUP * HD), jnp.bfloat16)],
            input_output_aliases={7: 0, 8: 1, 9: 2},
            compiler_params=params(),
            cost_estimate=cost,
            name="step",
        )(info, queries, *received, here_a, here_b, *state)

    packed = pl.pallas_call(
        finish_kernel,
        out_shape=jax.ShapeDtypeStruct((NY * NC, ROWS // NC, PACK), jnp.bfloat16),
        in_specs=[SMEM_SPEC] + [VMEM_SPEC] * 3,
        out_specs=VMEM_SPEC,
        compiler_params=params(),
        name="finish",
    )(info, *state)
    parts = lax.all_to_all(packed, ("y", "core"), 0, 0, tiled=True)

    width = 1024
    mixed = pl.pallas_call(
        project_kernel,
        out_shape=jax.ShapeDtypeStruct((ROWS // NC, w_out.shape[1]), jnp.bfloat16),
        grid=(w_out.shape[1] // width,),
        in_specs=[
            SMEM_SPEC,
            VMEM_SPEC,
            pl.BlockSpec((GROUP * HD, width), lambda i: (0, i)),
            pl.BlockSpec((GROUP * HD, width), lambda i: (0, i)),
        ],
        out_specs=pl.BlockSpec((ROWS // NC, width), lambda i: (0, i)),
        scratch_shapes=[pltpu.VMEM((NC, ROWS // NC, GROUP * HD), jnp.bfloat16)],
        compiler_params=params(),
        name="project",
    )(info, parts, w_out, other_w)
    pieces = lax.all_to_all(mixed.reshape(NX, 32, -1), "x", 0, 0, tiled=True)
    return jnp.sum(pieces.astype(jnp.float32), axis=0).astype(jnp.bfloat16)


def solution(mesh):
    grid = Mesh(mesh.devices.reshape(NY, NZ, NX, NC), ("y", "z", "x", "core"))
    tokens, heads = ("y", "z"), ("x", "core")
    split = P(tokens, heads)
    return jax.shard_map(
        body,
        mesh=grid,
        in_specs=(split, split, split, P(), P(), P(), P(heads, None)),
        out_specs=P(tokens + heads, None),
        check_vma=False,
    )
```

```python
import functools
import math

import jax
import jax.numpy as jnp
from jax import lax
from jax.experimental import pallas as pl
from jax.experimental.pallas import tpu as pltpu
from jax.sharding import Mesh
from jax.sharding import PartitionSpec as P


HD = 128
GROUP = 4
NY, NZ, NX, NC = 4, 16, 4, 2
ROWS = 256
ROW_KEYS = NZ * ROWS
LOW = -1e30
MASKED = -3e30
SCALE = 1.0 / math.sqrt(HD)
EXP2_SCALE = SCALE * math.log2(math.e)
STAT_ROWS = 16
PACK = GROUP * HD + STAT_ROWS
NT = (((1,), (1,)), ((), ()))


def pack_kernel(k_ref, v_ref, out_ref):
    out_ref[:, :HD] = k_ref[...]
    for half in range(2):
        rows = slice(half * HD, (half + 1) * HD)
        out_ref[rows, HD:] = v_ref[rows, :].astype(jnp.float32).T.astype(jnp.bfloat16)


def order_kernel(q_ref, out_ref):
    for x in range(NX):
        for c in range(NC):
            to, at = c * 128 + x * 32, (x * NC + c) * 32
            out_ref[to : to + 32, :] = q_ref[at : at + 32, :]


def query_offsets(shape):
    col = lax.broadcasted_iota(jnp.int32, shape, 1)
    return ((col % 128) // 32 * NC + col // 128) * 32 + col % 32


def fold(q_ref, slot, keys, values, mask, valid, acc, top, total):
    def score(h):
        q = q_ref[slot, :, h * HD : (h + 1) * HD]
        out = []
        for k in keys:
            s = lax.dot_general(k, q, NT, preferred_element_type=jnp.float32)
            out.append(s if mask is None else jnp.where(mask, s, MASKED))
        return out

    def peaks(h, scores):
        new = top[slot, h]
        for n, s in enumerate(scores):
            peak = jnp.max(s.reshape(ROWS // 8, 8, ROWS), axis=0)
            peak = jnp.max(peak, axis=0, keepdims=True)
            if valid is not None:
                peak = jnp.where(valid[n], peak, LOW)
            new = jnp.maximum(new, peak)
        return new

    scores = score(0)
    new = peaks(0, scores)
    for h in range(GROUP):
        if h + 1 < GROUP:
            scores_next = score(h + 1)
            new_next = peaks(h + 1, scores_next)
        old = top[slot, h]
        factor = jnp.exp2((old - new) * EXP2_SCALE)
        part = total[slot, h] * factor
        weights = []
        for n, s in enumerate(scores):
            shift = new[:1] * EXP2_SCALE
            if valid is not None:
                shift = jnp.where(valid[n], shift, -MASKED)
            w = jnp.exp2(s * EXP2_SCALE - shift)
            part = part + jnp.sum(w.reshape(ROWS // 8, 8, ROWS), axis=0)
            weights.append(w.astype(jnp.bfloat16))
        out = jnp.dot(
            jnp.concatenate(values, axis=1),
            jnp.concatenate(weights, axis=0),
            preferred_element_type=jnp.float32,
        )
        top[slot, h] = new
        total[slot, h] = part
        acc[slot, h] = acc[slot, h] * factor[:1] + out
        if h + 1 < GROUP:
            scores, new = scores_next, new_next


def split_block(block_ref, k_ref, v_ref):
    k_ref[...] = block_ref[:, :HD]
    v_ref[:, :HD] = block_ref[:HD, HD:]
    v_ref[:, HD:] = block_ref[HD:, HD:]


def fold_masked(info, q_ref, slot, k_ref, v_ref, key_start, acc, top, total):
    kind, sink, window = info[2], info[3], info[4]
    query_start = (info[0] + slot) * ROW_KEYS + info[1] * ROWS
    needed = (key_start <= query_start + ROWS - 1) & (
        (kind == 1) | (key_start + ROWS - 1 > query_start - window) | (key_start < sink)
    )

    @pl.when(needed)
    def _():
        i = query_start + query_offsets((ROWS, ROWS))
        j = key_start + lax.broadcasted_iota(jnp.int32, (ROWS, ROWS), 0)
        mask = (j <= i) & ((kind == 1) | (j > i - window) | (j < sink))
        fold(q_ref, slot, [k_ref[...]], [v_ref[...]], mask, None, acc, top, total)


def first_kernel(kinds, sinks, windows, q_ref, own_ref, acc, top, total, k_ref, v_ref):
    info = read_info((kinds, sinks, windows))
    acc[...] = jnp.zeros_like(acc)
    top[...] = jnp.full_like(top, LOW)
    total[...] = jnp.zeros_like(total)
    own_start = info[0] * ROW_KEYS + info[1] * ROWS
    split_block(own_ref, k_ref, v_ref)
    fold_masked(info, q_ref, 0, k_ref, v_ref, own_start, acc, top, total)


def step_kernel(
    distance, last, kinds, sinks, windows, q0_ref, q1_ref, q2_ref, q3_ref, a_ref, b_ref,
    acc_in, top_in, total_in, acc, top, total, q_ref, k_ref, v_ref
):
    del acc_in, top_in, total_in
    info = read_info((kinds, sinks, windows))
    y, z, kind = info[0], info[1], info[2]
    slots = NY - y
    a_place = lax.rem(z - distance + NZ, NZ)
    b_place = lax.rem(z + (0 if last else distance), NZ)
    q_ref[0] = q0_ref[...]
    q_ref[1] = q1_ref[...]
    q_ref[2] = q2_ref[...]
    q_ref[3] = q3_ref[...]
    split_block(a_ref, k_ref.at[0], v_ref.at[0])
    split_block(b_ref, k_ref.at[1], v_ref.at[1])
    a_before = a_place < z
    b_before = b_place < z

    @pl.when(kind == 1)
    def _():
        @pl.loop(jnp.where(a_before | b_before, 0, 1), slots)
        def _(slot):
            valid = [(slot > 0) | a_before, (slot > 0) | b_before]
            fold(q_ref, slot, [k_ref[0], k_ref[1]], [v_ref[0], v_ref[1]], None, valid, acc, top, total)

    @pl.when(kind != 1)
    def _():
        @pl.loop(0, 2 * slots)
        def _(n):
            slot = n // 2
            side = n % 2
            place = jnp.where(side == 0, a_place, b_place)
            skip = (slot == 0) & (place == z)

            @pl.when(jnp.logical_not(skip))
            def _():
                key_start = y * ROW_KEYS + place * ROWS
                fold_masked(info, q_ref, slot, k_ref.at[side], v_ref.at[side], key_start, acc, top, total)


def finish_kernel(acc, top, total, out_ref):
    y = lax.axis_index("y")
    for target in range(NY):
        slot = jnp.maximum(target - y, 0)
        valid = target >= y
        parts = []
        for h in range(GROUP):
            s = jnp.sum(total[slot, h], axis=0, keepdims=True)
            have = (s > 0.0) & valid
            safe = jnp.where(have, s, 1.0)
            o = jnp.where(have, acc[slot, h] * (1.0 / safe), 0.0).astype(jnp.bfloat16)
            lse = jnp.where(have, top[slot, h][:1] * SCALE + jnp.log(safe), LOW)
            for c in range(NC):
                out_ref[target * NC + c, h * HD : (h + 1) * HD, :] = o[:, c * 128 : (c + 1) * 128]
            high = lse.astype(jnp.bfloat16).astype(jnp.float32)
            rest = lse - high
            mid = rest.astype(jnp.bfloat16).astype(jnp.float32)
            parts += [high, mid, rest - mid]
        parts += [jnp.zeros_like(parts[0])] * (STAT_ROWS - len(parts))
        packed = jnp.concatenate(parts, axis=0).astype(jnp.bfloat16)
        for c in range(NC):
            out_ref[target * NC + c, GROUP * HD :, :] = packed[:, c * 128 : (c + 1) * 128]


def project_kernel(parts_ref, own_w_ref, other_w_ref, out_ref, mix):
    @pl.when(pl.program_id(0) == 0)
    def _():
        core = lax.axis_index("core")
        for side in range(NC):
            source = core if side == 0 else 1 - core
            stats = [
                parts_ref[y * NC + source, GROUP * HD :, :].astype(jnp.float32) for y in range(NY)
            ]
            for h in range(GROUP):
                lse = [s[3 * h : 3 * h + 1] + s[3 * h + 1 : 3 * h + 2] + s[3 * h + 2 : 3 * h + 3] for s in stats]
                peak = functools.reduce(jnp.maximum, lse)
                weight = [jnp.exp(v - peak) for v in lse]
                norm = 1.0 / functools.reduce(jnp.add, weight)
                out = None
                for y in range(NY):
                    o = parts_ref[y * NC + source, h * HD : (h + 1) * HD, :].astype(jnp.float32)
                    o = o * (weight[y] * norm)
                    out = o if out is None else out + o
                mix[side, :, h * HD : (h + 1) * HD] = out.T.astype(jnp.bfloat16)

    out_ref[...] = (
        jnp.dot(mix[0], own_w_ref[...], preferred_element_type=jnp.float32)
        + jnp.dot(mix[1], other_w_ref[...], preferred_element_type=jnp.float32)
    ).astype(jnp.bfloat16)


def read_info(heads):
    y, z = lax.axis_index("y"), lax.axis_index("z")
    core = lax.axis_index("core")
    head = lax.axis_index("x") * NC + core
    return (y, z, *(table[head] for table in heads), core)


VMEM_SPEC = pl.BlockSpec(memory_space=pltpu.VMEM)
SMEM_SPEC = pl.BlockSpec(memory_space=pltpu.SMEM)
STATE = [
    jax.ShapeDtypeStruct((NY, GROUP, HD, ROWS), jnp.float32),
    jax.ShapeDtypeStruct((NY, GROUP, 8, ROWS), jnp.float32),
    jax.ShapeDtypeStruct((NY, GROUP, 8, ROWS), jnp.float32),
]


def params(mib=24):
    return pltpu.CompilerParams(vmem_limit_bytes=mib << 20)


def body(queries, keys, values, head_kind, sink_len, window_len, w_out):
    heads = (head_kind, sink_len, window_len)
    own = pl.pallas_call(
        pack_kernel,
        out_shape=jax.ShapeDtypeStruct((ROWS, 2 * HD), jnp.bfloat16),
        in_specs=[VMEM_SPEC] * 2,
        out_specs=VMEM_SPEC,
        compiler_params=params(),
        name="pack",
    )(keys, values)
    queries = pl.pallas_call(
        order_kernel,
        out_shape=jax.ShapeDtypeStruct(queries.shape, jnp.bfloat16),
        in_specs=[VMEM_SPEC],
        out_specs=VMEM_SPEC,
        compiler_params=params(),
        name="order",
    )(queries)

    ahead = [(i, (i + 1) % NZ) for i in range(NZ)]
    behind = [(i, (i - 1) % NZ) for i in range(NZ)]
    half = NZ // 2
    a, b = {0: own}, {0: own}
    cost = pl.CostEstimate(flops=1 << 30, bytes_accessed=8 << 20, transcendentals=1 << 22)
    state = pl.pallas_call(
        first_kernel,
        out_shape=STATE,
        in_specs=[SMEM_SPEC] * 3 + [VMEM_SPEC] * 2,
        out_specs=[VMEM_SPEC] * 3,
        scratch_shapes=[pltpu.VMEM((ROWS, HD), jnp.bfloat16), pltpu.VMEM((HD, ROWS), jnp.bfloat16)],
        compiler_params=params(),
        cost_estimate=cost,
        name="first",
    )(*heads, queries[None], own)

    for d in range(1, half + 1):
        a[d] = lax.ppermute(a[d - 1], "z", ahead)
        if d < half:
            b[d] = lax.ppermute(b[d - 1], "z", behind)
    b[half] = own
    received = []
    for k in range(1, NY):
        received.append(lax.ppermute(queries, "y", [(i, i - k) for i in range(k, NY)]))
    other_w = lax.ppermute(w_out, "core", [(0, 1), (1, 0)])

    for d in range(1, half + 1):
        state = pl.pallas_call(
            functools.partial(step_kernel, d, d == half),
            out_shape=STATE,
            in_specs=[SMEM_SPEC] * 3 + [VMEM_SPEC] * 9,
            out_specs=[VMEM_SPEC] * 3,
            scratch_shapes=[
                pltpu.VMEM((NY, ROWS, GROUP * HD), jnp.bfloat16),
                pltpu.VMEM((2, ROWS, HD), jnp.bfloat16),
                pltpu.VMEM((2, HD, ROWS), jnp.bfloat16),
            ],
            input_output_aliases={9: 0, 10: 1, 11: 2},
            compiler_params=params(),
            cost_estimate=cost,
            name="step",
        )(*heads, queries, *received, a[d], b[d], *state)

    packed = pl.pallas_call(
        finish_kernel,
        out_shape=jax.ShapeDtypeStruct((NY * NC, PACK, ROWS // NC), jnp.bfloat16),
        in_specs=[VMEM_SPEC] * 3,
        out_specs=VMEM_SPEC,
        compiler_params=params(),
        name="finish",
    )(*state)
    parts = lax.all_to_all(packed, ("y", "core"), 0, 0, tiled=True)

    width = 1024
    mixed = pl.pallas_call(
        project_kernel,
        out_shape=jax.ShapeDtypeStruct((ROWS // NC, w_out.shape[1]), jnp.bfloat16),
        grid=(w_out.shape[1] // width,),
        in_specs=[
            VMEM_SPEC,
            pl.BlockSpec((GROUP * HD, width), lambda i: (0, i)),
            pl.BlockSpec((GROUP * HD, width), lambda i: (0, i)),
        ],
        out_specs=pl.BlockSpec((ROWS // NC, width), lambda i: (0, i)),
        scratch_shapes=[pltpu.VMEM((NC, ROWS // NC, GROUP * HD), jnp.bfloat16)],
        compiler_params=params(),
        name="project",
    )(parts, w_out, other_w)
    pieces = lax.all_to_all(mixed.reshape(NX, 32, -1), "x", 0, 0, tiled=True)
    return jnp.sum(pieces.astype(jnp.float32), axis=0).astype(jnp.bfloat16)


def solution(mesh):
    grid = Mesh(mesh.devices.reshape(NY, NZ, NX, NC), ("y", "z", "x", "core"))
    tokens, heads = ("y", "z"), ("x", "core")
    split = P(tokens, heads)

    return jax.shard_map(
        body,
        mesh=grid,
        in_specs=(split, split, split, P(), P(), P(), P(heads, None)),
        out_specs=P(tokens + heads, None),
        check_vma=False,
    )
```

```python
import functools
import math

import jax
import jax.numpy as jnp
from jax import lax
from jax.experimental import pallas as pl
from jax.experimental.pallas import tpu as pltpu
from jax.sharding import Mesh
from jax.sharding import PartitionSpec as P


HD = 128
GROUP = 4
NY, NZ, NX, NC = 4, 16, 4, 2
ROWS = 256
ROW_KEYS = NZ * ROWS
LOW = -1e30
MASKED = -3e30
SCALE = 1.0 / math.sqrt(HD)
EXP2_SCALE = SCALE * math.log2(math.e)
LN2 = math.log(2.0)
STAT_ROWS = 16
PACK = GROUP * HD + STAT_ROWS
NT = (((1,), (1,)), ((), ()))


def pack_kernel(k_ref, v_ref, out_ref):
    out_ref[:, :HD] = k_ref[...]
    for half in range(2):
        rows = slice(half * HD, (half + 1) * HD)
        out_ref[rows, HD:] = v_ref[rows, :].astype(jnp.float32).T.astype(jnp.bfloat16)


def order_kernel(q_ref, out_ref):
    for x in range(NX):
        for c in range(NC):
            to, at = c * 128 + x * 32, (x * NC + c) * 32
            out_ref[to : to + 32, :] = q_ref[at : at + 32, :]


def query_offsets(shape):
    col = lax.broadcasted_iota(jnp.int32, shape, 1)
    return ((col % 128) // 32 * NC + col // 128) * 32 + col % 32


def fold(q_ref, slot, keys, values, mask, valid, acc, top, total):
    def score(h):
        q = q_ref[slot, :, 2 * h * HD : 2 * (h + 1) * HD]
        out = []
        for k in keys:
            s = lax.dot_general(k, q, NT, preferred_element_type=jnp.float32)
            out.append(s if mask is None else jnp.where(mask, s, MASKED))
        return out

    def peaks(h, scores):
        new = top[slot, h]
        for n, s in enumerate(scores):
            peak = jnp.max(s.reshape(ROWS // 8, 8, ROWS), axis=0)
            peak = jnp.max(peak, axis=0, keepdims=True)
            if valid is not None:
                peak = jnp.where(valid[n], peak, LOW)
            new = jnp.maximum(new, peak)
        return new

    scores = score(0)
    new = peaks(0, scores)
    for h in range(GROUP):
        if h + 1 < GROUP:
            scores_next = score(h + 1)
            new_next = peaks(h + 1, scores_next)
        old = top[slot, h]
        factor = jnp.exp2(old - new)
        part = total[slot, h] * factor
        weights = []
        for n, s in enumerate(scores):
            shift = new[:1]
            if valid is not None:
                shift = jnp.where(valid[n], shift, -MASKED)
            w = jnp.exp2(s - shift)
            part = part + jnp.sum(w.reshape(ROWS // 8, 8, ROWS), axis=0)
            weights.append(w.astype(jnp.bfloat16))
        out = jnp.dot(
            jnp.concatenate(values, axis=1),
            jnp.concatenate(weights, axis=0),
            preferred_element_type=jnp.float32,
        )
        top[slot, h] = new
        total[slot, h] = part
        acc[slot, h] = acc[slot, h] * factor[:1] + out
        if h + 1 < GROUP:
            scores, new = scores_next, new_next


def split_block(block_ref, k_ref, v_ref):
    k_ref[:, :HD] = block_ref[:, :HD]
    k_ref[:, HD:] = block_ref[:, :HD]
    v_ref[:, :HD] = block_ref[:HD, HD:]
    v_ref[:, HD:] = block_ref[HD:, HD:]


def fold_masked(info, q_ref, slot, local, k_ref, v_ref, key_start, acc, top, total):
    kind, sink, window = info[2], info[3], info[4]
    query_start = (info[0] + slot) * ROW_KEYS + info[1] * ROWS
    needed = (key_start <= query_start + ROWS - 1) & (
        (kind == 1) | (key_start + ROWS - 1 > query_start - window) | (key_start < sink)
    )

    @pl.when(needed)
    def _():
        i = query_start + query_offsets((ROWS, ROWS))
        j = key_start + lax.broadcasted_iota(jnp.int32, (ROWS, ROWS), 0)
        mask = (j <= i) & ((kind == 1) | (j > i - window) | (j < sink))
        fold(q_ref, local, [k_ref[...]], [v_ref[...]], mask, None, acc, top, total)


def scale_queries(q_ref, out_ref, local):
    for h in range(GROUP):
        scaled = q_ref[:, h * HD : (h + 1) * HD].astype(jnp.float32) * EXP2_SCALE
        high = scaled.astype(jnp.bfloat16)
        out_ref[local, :, 2 * h * HD : (2 * h + 1) * HD] = high
        rest = scaled - high.astype(jnp.float32)
        out_ref[local, :, (2 * h + 1) * HD : 2 * (h + 1) * HD] = rest.astype(jnp.bfloat16)


def first_kernel(
    kinds, sinks, windows, q_ref, own_ref, scaled, acc, top, total, acc1, top1, total1, k_ref, v_ref
):
    info = read_info((kinds, sinks, windows))
    for state in ((acc, top, total), (acc1, top1, total1)):
        state[0][...] = jnp.zeros_like(state[0])
        state[1][...] = jnp.full_like(state[1], LOW)
        state[2][...] = jnp.zeros_like(state[2])
    scale_queries(q_ref, scaled, 0)
    own_start = info[0] * ROW_KEYS + info[1] * ROWS
    split_block(own_ref, k_ref, v_ref)
    fold_masked(info, scaled, 0, 0, k_ref, v_ref, own_start, acc, top, total)


def join_kernel(scaled_ref, q1_ref, out_ref):
    out_ref[0] = scaled_ref[0]
    scale_queries(q1_ref, out_ref, 1)


def pair_kernel(q2_ref, q3_ref, out_ref):
    scale_queries(q2_ref, out_ref, 0)
    scale_queries(q3_ref, out_ref, 1)


def step_kernel(
    distance, last, part, kinds, sinks, windows, q_ref, a_ref, b_ref,
    acc_in, top_in, total_in, acc, top, total, k_ref, v_ref
):
    del acc_in, top_in, total_in
    info = read_info((kinds, sinks, windows))
    y, z, kind = info[0], info[1], info[2]
    base = 2 * part
    count = jnp.clip(NY - y - base, 0, 2)
    a_place = lax.rem(z - distance + NZ, NZ)
    b_place = lax.rem(z + (0 if last else distance), NZ)
    a_before = a_place < z
    b_before = b_place < z

    @pl.when(count > 0)
    def _():
        split_block(a_ref, k_ref.at[0], v_ref.at[0])
        split_block(b_ref, k_ref.at[1], v_ref.at[1])

    @pl.when(kind == 1)
    def _():
        first = 0 if part else jnp.where(a_before | b_before, 0, 1)

        @pl.loop(first, count)
        def _(n):
            valid = None if part else [(n > 0) | a_before, (n > 0) | b_before]
            fold(q_ref, n, [k_ref[0], k_ref[1]], [v_ref[0], v_ref[1]], None, valid, acc, top, total)

    @pl.when(kind != 1)
    def _():
        @pl.loop(0, 2 * count)
        def _(n):
            local = n // 2
            side = n % 2
            slot = base + local
            place = jnp.where(side == 0, a_place, b_place)
            skip = (slot == 0) & (place == z)

            @pl.when(jnp.logical_not(skip))
            def _():
                key_start = y * ROW_KEYS + place * ROWS
                fold_masked(
                    info, q_ref, slot, local, k_ref.at[side], v_ref.at[side], key_start, acc, top, total
                )


def finish_kernel(acc0, top0, total0, acc1, top1, total1, out_ref):
    y = lax.axis_index("y")

    @pl.loop(0, y * NC)
    def _(piece):
        out_ref[piece, : GROUP * HD] = jnp.zeros((GROUP * HD, 128), jnp.bfloat16)
        out_ref[piece, GROUP * HD :] = jnp.full((STAT_ROWS, 128), LOW, jnp.bfloat16)

    def send(slot):
        local = slot % 2
        acc, top, total = ((acc0, top0, total0), (acc1, top1, total1))[slot // 2]
        parts = []
        for h in range(GROUP):
            s = jnp.sum(total[local, h], axis=0, keepdims=True)
            have = s > 0.0
            safe = jnp.where(have, s, 1.0)
            o = (acc[local, h] * (1.0 / safe)).astype(jnp.bfloat16)
            lse = jnp.where(have, top[local, h][:1] * LN2 + jnp.log(safe), LOW)
            for c in range(NC):
                out_ref[(y + slot) * NC + c, h * HD : (h + 1) * HD, :] = o[:, c * 128 : (c + 1) * 128]
            high = lse.astype(jnp.bfloat16).astype(jnp.float32)
            rest = lse - high
            mid = rest.astype(jnp.bfloat16).astype(jnp.float32)
            parts += [high, mid, rest - mid]
        parts += [jnp.zeros_like(parts[0])] * (STAT_ROWS - len(parts))
        packed = jnp.concatenate(parts, axis=0).astype(jnp.bfloat16)
        for c in range(NC):
            out_ref[(y + slot) * NC + c, GROUP * HD :, :] = packed[:, c * 128 : (c + 1) * 128]

    send(0)
    for slot in range(1, NY):
        pl.when(slot < NY - y)(functools.partial(send, slot))


def project_kernel(parts_ref, own_w_ref, other_w_ref, out_ref, mix):
    @pl.when(pl.program_id(0) == 0)
    def _():
        core = lax.axis_index("core")
        for side in range(NC):
            source = core if side == 0 else 1 - core
            stats = [
                parts_ref[y * NC + source, GROUP * HD :, :].astype(jnp.float32) for y in range(NY)
            ]
            for h in range(GROUP):
                lse = [s[3 * h : 3 * h + 1] + s[3 * h + 1 : 3 * h + 2] + s[3 * h + 2 : 3 * h + 3] for s in stats]
                peak = functools.reduce(jnp.maximum, lse)
                weight = [jnp.exp(v - peak) for v in lse]
                norm = 1.0 / functools.reduce(jnp.add, weight)
                out = None
                for y in range(NY):
                    o = parts_ref[y * NC + source, h * HD : (h + 1) * HD, :].astype(jnp.float32)
                    o = o * (weight[y] * norm)
                    out = o if out is None else out + o
                mix[side, :, h * HD : (h + 1) * HD] = out.T.astype(jnp.bfloat16)

    out_ref[...] = (
        jnp.dot(mix[0], own_w_ref[...], preferred_element_type=jnp.float32)
        + jnp.dot(mix[1], other_w_ref[...], preferred_element_type=jnp.float32)
    ).astype(jnp.bfloat16)


def read_info(heads):
    y, z = lax.axis_index("y"), lax.axis_index("z")
    core = lax.axis_index("core")
    head = lax.axis_index("x") * NC + core
    return (y, z, *(table[head] for table in heads), core)


VMEM_SPEC = pl.BlockSpec(memory_space=pltpu.VMEM)
SMEM_SPEC = pl.BlockSpec(memory_space=pltpu.SMEM)
STATE = [
    jax.ShapeDtypeStruct((2, GROUP, HD, ROWS), jnp.float32),
    jax.ShapeDtypeStruct((2, GROUP, 8, ROWS), jnp.float32),
    jax.ShapeDtypeStruct((2, GROUP, 8, ROWS), jnp.float32),
]


def params(mib=24):
    return pltpu.CompilerParams(vmem_limit_bytes=mib << 20)


def body(queries, keys, values, head_kind, sink_len, window_len, w_out):
    heads = (head_kind, sink_len, window_len)
    own = pl.pallas_call(
        pack_kernel,
        grid=(1,),
        out_shape=jax.ShapeDtypeStruct((ROWS, 2 * HD), jnp.bfloat16),
        in_specs=[pl.BlockSpec((ROWS, HD), lambda i: (0, 0))] * 2,
        out_specs=VMEM_SPEC,
        compiler_params=params(),
        name="pack",
    )(keys, values)
    queries = pl.pallas_call(
        order_kernel,
        grid=(1,),
        out_shape=jax.ShapeDtypeStruct(queries.shape, jnp.bfloat16),
        in_specs=[pl.BlockSpec(queries.shape, lambda i: (0, 0))],
        out_specs=VMEM_SPEC,
        compiler_params=params(),
        name="order",
    )(queries)

    ahead = [(i, (i + 1) % NZ) for i in range(NZ)]
    behind = [(i, (i - 1) % NZ) for i in range(NZ)]
    half = NZ // 2
    a, b = {0: own}, {0: own}
    cost = pl.CostEstimate(flops=1 << 30, bytes_accessed=8 << 20, transcendentals=1 << 22)
    scaled_type = jax.ShapeDtypeStruct((2, ROWS, 2 * GROUP * HD), jnp.bfloat16)
    scaled, *state = pl.pallas_call(
        first_kernel,
        out_shape=[scaled_type] + STATE * 2,
        in_specs=[SMEM_SPEC] * 3 + [VMEM_SPEC] * 2,
        out_specs=[VMEM_SPEC] * 7,
        scratch_shapes=[
            pltpu.VMEM((ROWS, 2 * HD), jnp.bfloat16),
            pltpu.VMEM((HD, ROWS), jnp.bfloat16),
        ],
        compiler_params=params(),
        cost_estimate=cost,
        name="first",
    )(*heads, queries, own)
    states = [state[:3], state[3:]]

    for d in range(1, half + 1):
        a[d] = lax.ppermute(a[d - 1], "z", ahead)
        if d < half:
            b[d] = lax.ppermute(b[d - 1], "z", behind)
    b[half] = own
    received = []
    for k in range(1, NY):
        received.append(lax.ppermute(queries, "y", [(i, i - k) for i in range(k, NY)]))
    other_w = lax.ppermute(w_out, "core", [(0, 1), (1, 0)])

    slots = [
        pl.pallas_call(
            kernel,
            out_shape=scaled_type,
            in_specs=[VMEM_SPEC] * 2,
            out_specs=VMEM_SPEC,
            compiler_params=params(),
        )(*operands)
        for kernel, operands in ((join_kernel, (scaled, received[0])), (pair_kernel, received[1:]))
    ]
    for d in range(1, half + 1):
        for part in range(2):
            states[part] = pl.pallas_call(
                functools.partial(step_kernel, d, d == half, part),
                out_shape=STATE,
                in_specs=[SMEM_SPEC] * 3 + [VMEM_SPEC] * 6,
                out_specs=[VMEM_SPEC] * 3,
                scratch_shapes=[
                    pltpu.VMEM((2, ROWS, 2 * HD), jnp.bfloat16),
                    pltpu.VMEM((2, HD, ROWS), jnp.bfloat16),
                ],
                input_output_aliases={6: 0, 7: 1, 8: 2},
                compiler_params=params(),
                cost_estimate=cost,
                name="step",
            )(*heads, slots[part], a[d], b[d], *states[part])

    packed = pl.pallas_call(
        finish_kernel,
        out_shape=jax.ShapeDtypeStruct((NY * NC, PACK, ROWS // NC), jnp.bfloat16),
        in_specs=[VMEM_SPEC] * 6,
        out_specs=VMEM_SPEC,
        compiler_params=params(),
        name="finish",
    )(*states[0], *states[1])
    parts = lax.all_to_all(packed, ("y", "core"), 0, 0, tiled=True)

    width = 1024
    mixed = pl.pallas_call(
        project_kernel,
        out_shape=jax.ShapeDtypeStruct((ROWS // NC, w_out.shape[1]), jnp.bfloat16),
        grid=(w_out.shape[1] // width,),
        in_specs=[
            VMEM_SPEC,
            pl.BlockSpec((GROUP * HD, width), lambda i: (0, i)),
            pl.BlockSpec((GROUP * HD, width), lambda i: (0, i)),
        ],
        out_specs=pl.BlockSpec((ROWS // NC, width), lambda i: (0, i)),
        scratch_shapes=[pltpu.VMEM((NC, ROWS // NC, GROUP * HD), jnp.bfloat16)],
        compiler_params=params(),
        name="project",
    )(parts, w_out, other_w)
    pieces = lax.all_to_all(mixed.reshape(NX, 32, -1), "x", 0, 0, tiled=True)
    return jnp.sum(pieces.astype(jnp.float32), axis=0).astype(jnp.bfloat16)


def solution(mesh):
    grid = Mesh(mesh.devices.reshape(NY, NZ, NX, NC), ("y", "z", "x", "core"))
    tokens, heads = ("y", "z"), ("x", "core")
    split = P(tokens, heads)

    return jax.shard_map(
        body,
        mesh=grid,
        in_specs=(split, split, split, P(), P(), P(), P(heads, None)),
        out_specs=P(tokens + heads, None),
        check_vma=False,
    )
```

```python
import functools
import math

import jax
import jax.numpy as jnp
from jax import lax
from jax.experimental import pallas as pl
from jax.experimental.pallas import tpu as pltpu
from jax.sharding import Mesh
from jax.sharding import PartitionSpec as P


HD = 128
GROUP = 4
NY, NZ, NX, NC = 4, 16, 4, 2
ROWS = 256
ROW_KEYS = NZ * ROWS
LOW = -1e30
MASKED = -3e30
SCALE = 1.0 / math.sqrt(HD)
EXP2_SCALE = SCALE * math.log2(math.e)
STAT_ROWS = 16
PACK = GROUP * HD + STAT_ROWS
NT = (((1,), (1,)), ((), ()))


def pack_kernel(k_ref, v_ref, out_ref):
    out_ref[:, :HD] = k_ref[...]
    for half in range(2):
        rows = slice(half * HD, (half + 1) * HD)
        out_ref[rows, HD:] = v_ref[rows, :].astype(jnp.float32).T.astype(jnp.bfloat16)


def order_kernel(q_ref, out_ref):
    for x in range(NX):
        for c in range(NC):
            to, at = c * 128 + x * 32, (x * NC + c) * 32
            out_ref[to : to + 32, :] = q_ref[at : at + 32, :]


def query_offsets(shape):
    col = lax.broadcasted_iota(jnp.int32, shape, 1)
    return ((col % 128) // 32 * NC + col // 128) * 32 + col % 32


def fold(q_ref, slot, keys, values, mask, valid, acc, top, total):
    def score(h):
        q = q_ref[slot, :, h * HD : (h + 1) * HD]
        out = []
        for k in keys:
            s = lax.dot_general(k, q, NT, preferred_element_type=jnp.float32)
            out.append(s if mask is None else jnp.where(mask, s, MASKED))
        return out

    def peaks(h, scores):
        new = top[slot, h]
        for n, s in enumerate(scores):
            peak = jnp.max(s.reshape(ROWS // 8, 8, ROWS), axis=0)
            peak = jnp.max(peak, axis=0, keepdims=True)
            if valid is not None:
                peak = jnp.where(valid[n], peak, LOW)
            new = jnp.maximum(new, peak)
        return new

    scores = score(0)
    new = peaks(0, scores)
    for h in range(GROUP):
        if h + 1 < GROUP:
            scores_next = score(h + 1)
            new_next = peaks(h + 1, scores_next)
        old = top[slot, h]
        factor = jnp.exp2((old - new) * EXP2_SCALE)
        part = total[slot, h] * factor
        weights = []
        for n, s in enumerate(scores):
            shift = new[:1] * EXP2_SCALE
            if valid is not None:
                shift = jnp.where(valid[n], shift, -MASKED)
            w = jnp.exp2(s * EXP2_SCALE - shift)
            part = part + jnp.sum(w.reshape(ROWS // 8, 8, ROWS), axis=0)
            weights.append(w.astype(jnp.bfloat16))
        out = jnp.dot(
            jnp.concatenate(values, axis=1),
            jnp.concatenate(weights, axis=0),
            preferred_element_type=jnp.float32,
        )
        top[slot, h] = new
        total[slot, h] = part
        acc[slot, h] = acc[slot, h] * factor[:1] + out
        if h + 1 < GROUP:
            scores, new = scores_next, new_next


def split_block(block_ref, k_ref, v_ref):
    k_ref[...] = block_ref[:, :HD]
    v_ref[:, :HD] = block_ref[:HD, HD:]
    v_ref[:, HD:] = block_ref[HD:, HD:]


def fold_masked(info, q_ref, slot, k_ref, v_ref, key_start, acc, top, total):
    kind, sink, window = info[2], info[3], info[4]
    query_start = (info[0] + slot) * ROW_KEYS + info[1] * ROWS
    needed = (key_start <= query_start + ROWS - 1) & (
        (kind == 1) | (key_start + ROWS - 1 > query_start - window) | (key_start < sink)
    )

    @pl.when(needed)
    def _():
        i = query_start + query_offsets((ROWS, ROWS))
        j = key_start + lax.broadcasted_iota(jnp.int32, (ROWS, ROWS), 0)
        mask = (j <= i) & ((kind == 1) | (j > i - window) | (j < sink))
        fold(q_ref, slot, [k_ref[...]], [v_ref[...]], mask, None, acc, top, total)


def first_kernel(kinds, sinks, windows, q_ref, own_ref, acc, top, total, k_ref, v_ref):
    info = read_info((kinds, sinks, windows))
    acc[...] = jnp.zeros_like(acc)
    top[...] = jnp.full_like(top, LOW)
    total[...] = jnp.zeros_like(total)
    own_start = info[0] * ROW_KEYS + info[1] * ROWS
    split_block(own_ref, k_ref, v_ref)
    fold_masked(info, q_ref, 0, k_ref, v_ref, own_start, acc, top, total)


def stack_kernel(q0_ref, q1_ref, q2_ref, q3_ref, out_ref):
    for slot, ref in enumerate((q0_ref, q1_ref, q2_ref, q3_ref)):
        out_ref[slot] = ref[...]


def step_kernel(
    distances, last, kinds, sinks, windows, q_ref, a_ref, b_ref,
    acc_in, top_in, total_in, acc, top, total, k_ref, v_ref
):
    del acc_in, top_in, total_in
    info = read_info((kinds, sinks, windows))
    y, z, kind = info[0], info[1], info[2]
    slots = NY - y
    places = []
    for i, distance in enumerate(distances):
        rows = pl.ds(i * ROWS, ROWS)
        split_block(a_ref.at[rows], k_ref.at[2 * i], v_ref.at[2 * i])
        split_block(b_ref.at[rows], k_ref.at[2 * i + 1], v_ref.at[2 * i + 1])
        places.append(lax.rem(z - distance + NZ, NZ))
        places.append(lax.rem(z + (0 if last else distance), NZ))
    before = [place < z for place in places]

    @pl.when(kind == 1)
    def _():
        any_before = functools.reduce(jnp.logical_or, before)

        @pl.loop(jnp.where(any_before, 0, 1), slots)
        def _(slot):
            for i in range(0, len(places), 2):
                sides = (i, i + 1)
                valid = [(slot > 0) | before[n] for n in sides]
                keys, values = [k_ref[n] for n in sides], [v_ref[n] for n in sides]
                fold(q_ref, slot, keys, values, None, valid, acc, top, total)

    @pl.when(kind != 1)
    def _():
        blocks = len(places)

        @pl.loop(0, blocks * slots)
        def _(n):
            slot = n // blocks
            side = n % blocks
            place = places[0]
            for i in range(1, blocks):
                place = jnp.where(side == i, places[i], place)
            skip = (slot == 0) & (place == z)

            @pl.when(jnp.logical_not(skip))
            def _():
                key_start = y * ROW_KEYS + place * ROWS
                fold_masked(
                    info, q_ref, slot, k_ref.at[side], v_ref.at[side], key_start, acc, top, total
                )


def finish_kernel(acc, top, total, out_ref):
    y = lax.axis_index("y")
    for target in range(NY):
        slot = jnp.maximum(target - y, 0)
        valid = target >= y
        parts = []
        for h in range(GROUP):
            s = jnp.sum(total[slot, h], axis=0, keepdims=True)
            have = (s > 0.0) & valid
            safe = jnp.where(have, s, 1.0)
            o = jnp.where(have, acc[slot, h] * (1.0 / safe), 0.0).astype(jnp.bfloat16)
            lse = jnp.where(have, top[slot, h][:1] * SCALE + jnp.log(safe), LOW)
            for c in range(NC):
                out_ref[target * NC + c, h * HD : (h + 1) * HD, :] = o[:, c * 128 : (c + 1) * 128]
            high = lse.astype(jnp.bfloat16).astype(jnp.float32)
            rest = lse - high
            mid = rest.astype(jnp.bfloat16).astype(jnp.float32)
            parts += [high, mid, rest - mid]
        parts += [jnp.zeros_like(parts[0])] * (STAT_ROWS - len(parts))
        packed = jnp.concatenate(parts, axis=0).astype(jnp.bfloat16)
        for c in range(NC):
            out_ref[target * NC + c, GROUP * HD :, :] = packed[:, c * 128 : (c + 1) * 128]


def project_kernel(parts_ref, own_w_ref, other_w_ref, out_ref, mix):
    @pl.when(pl.program_id(0) == 0)
    def _():
        core = lax.axis_index("core")
        for side in range(NC):
            source = core if side == 0 else 1 - core
            stats = [
                parts_ref[y * NC + source, GROUP * HD :, :].astype(jnp.float32) for y in range(NY)
            ]
            for h in range(GROUP):
                lse = [s[3 * h : 3 * h + 1] + s[3 * h + 1 : 3 * h + 2] + s[3 * h + 2 : 3 * h + 3] for s in stats]
                peak = functools.reduce(jnp.maximum, lse)
                weight = [jnp.exp(v - peak) for v in lse]
                norm = 1.0 / functools.reduce(jnp.add, weight)
                out = None
                for y in range(NY):
                    o = parts_ref[y * NC + source, h * HD : (h + 1) * HD, :].astype(jnp.float32)
                    o = o * (weight[y] * norm)
                    out = o if out is None else out + o
                mix[side, :, h * HD : (h + 1) * HD] = out.T.astype(jnp.bfloat16)

    out_ref[...] = (
        jnp.dot(mix[0], own_w_ref[...], preferred_element_type=jnp.float32)
        + jnp.dot(mix[1], other_w_ref[...], preferred_element_type=jnp.float32)
    ).astype(jnp.bfloat16)


def read_info(heads):
    y, z = lax.axis_index("y"), lax.axis_index("z")
    core = lax.axis_index("core")
    head = lax.axis_index("x") * NC + core
    return (y, z, *(table[head] for table in heads), core)


VMEM_SPEC = pl.BlockSpec(memory_space=pltpu.VMEM)
SMEM_SPEC = pl.BlockSpec(memory_space=pltpu.SMEM)
STATE = [
    jax.ShapeDtypeStruct((NY, GROUP, HD, ROWS), jnp.float32),
    jax.ShapeDtypeStruct((NY, GROUP, 8, ROWS), jnp.float32),
    jax.ShapeDtypeStruct((NY, GROUP, 8, ROWS), jnp.float32),
]


def params(mib=24):
    return pltpu.CompilerParams(vmem_limit_bytes=mib << 20)


ROUNDS = {1: (1, (1,)), 2: (2, (2, 3)), 3: (2, (4, 5)), 4: (2, (6, 7)), 5: (1, (8,))}


def body(queries, keys, values, head_kind, sink_len, window_len, w_out):
    heads = (head_kind, sink_len, window_len)
    own = pl.pallas_call(
        pack_kernel,
        grid=(1,),
        out_shape=jax.ShapeDtypeStruct((ROWS, 2 * HD), jnp.bfloat16),
        in_specs=[pl.BlockSpec((ROWS, HD), lambda i: (0, 0))] * 2,
        out_specs=VMEM_SPEC,
        compiler_params=params(),
        name="pack",
    )(keys, values)
    queries = pl.pallas_call(
        order_kernel,
        out_shape=jax.ShapeDtypeStruct(queries.shape, jnp.bfloat16),
        in_specs=[VMEM_SPEC],
        out_specs=VMEM_SPEC,
        compiler_params=params(),
        name="order",
    )(queries)

    a, b = {0: own}, {0: own}
    cost = pl.CostEstimate(flops=1 << 30, bytes_accessed=8 << 20, transcendentals=1 << 22)
    state = pl.pallas_call(
        first_kernel,
        out_shape=STATE,
        in_specs=[SMEM_SPEC] * 3 + [VMEM_SPEC] * 2,
        out_specs=[VMEM_SPEC] * 3,
        scratch_shapes=[pltpu.VMEM((ROWS, HD), jnp.bfloat16), pltpu.VMEM((HD, ROWS), jnp.bfloat16)],
        compiler_params=params(),
        cost_estimate=cost,
        name="first",
    )(*heads, queries[None], own)

    final = len(ROUNDS)
    send_a = send_b = own
    for d, (hops, _) in ROUNDS.items():
        a[d] = lax.ppermute(send_a, "z", [(i, (i + hops) % NZ) for i in range(NZ)])
        send_a = jnp.concatenate([own, a[1]], axis=0) if d == 1 else a[d]
        if d == final:
            b[d] = own
            break
        b[d] = lax.ppermute(send_b, "z", [(i, (i - hops) % NZ) for i in range(NZ)])
        send_b = jnp.concatenate([own, b[1]], axis=0) if d == 1 else b[d]
        if d + 1 == final:
            send_a = a[d][ROWS:]
    received = []
    for k in range(1, NY):
        received.append(lax.ppermute(queries, "y", [(i, i - k) for i in range(k, NY)]))
    other_w = lax.ppermute(w_out, "core", [(0, 1), (1, 0)])

    slots = pl.pallas_call(
        stack_kernel,
        out_shape=jax.ShapeDtypeStruct((NY, ROWS, GROUP * HD), jnp.bfloat16),
        in_specs=[VMEM_SPEC] * NY,
        out_specs=VMEM_SPEC,
        compiler_params=params(),
        name="stack",
    )(queries, *received)
    for d, (_, distances) in ROUNDS.items():
        state = pl.pallas_call(
            functools.partial(step_kernel, distances, d == final),
            out_shape=STATE,
            in_specs=[SMEM_SPEC] * 3 + [VMEM_SPEC] * 6,
            out_specs=[VMEM_SPEC] * 3,
            scratch_shapes=[
                pltpu.VMEM((2 * len(distances), ROWS, HD), jnp.bfloat16),
                pltpu.VMEM((2 * len(distances), HD, ROWS), jnp.bfloat16),
            ],
            input_output_aliases={6: 0, 7: 1, 8: 2},
            compiler_params=params(),
            cost_estimate=cost,
            name="step",
        )(*heads, slots, a[d], b[d], *state)

    packed = pl.pallas_call(
        finish_kernel,
        out_shape=jax.ShapeDtypeStruct((NY * NC, PACK, ROWS // NC), jnp.bfloat16),
        in_specs=[VMEM_SPEC] * 3,
        out_specs=VMEM_SPEC,
        compiler_params=params(),
        name="finish",
    )(*state)
    parts = lax.all_to_all(packed, ("y", "core"), 0, 0, tiled=True)

    width = 1024
    mixed = pl.pallas_call(
        project_kernel,
        out_shape=jax.ShapeDtypeStruct((ROWS // NC, w_out.shape[1]), jnp.bfloat16),
        grid=(w_out.shape[1] // width,),
        in_specs=[
            VMEM_SPEC,
            pl.BlockSpec((GROUP * HD, width), lambda i: (0, i)),
            pl.BlockSpec((GROUP * HD, width), lambda i: (0, i)),
        ],
        out_specs=pl.BlockSpec((ROWS // NC, width), lambda i: (0, i)),
        scratch_shapes=[pltpu.VMEM((NC, ROWS // NC, GROUP * HD), jnp.bfloat16)],
        compiler_params=params(),
        name="project",
    )(parts, w_out, other_w)
    pieces = lax.all_to_all(mixed.reshape(NX, 32, -1), "x", 0, 0, tiled=True)
    return jnp.sum(pieces.astype(jnp.float32), axis=0).astype(jnp.bfloat16)


def solution(mesh):
    grid = Mesh(mesh.devices.reshape(NY, NZ, NX, NC), ("y", "z", "x", "core"))
    tokens, heads = ("y", "z"), ("x", "core")
    split = P(tokens, heads)

    return jax.shard_map(
        body,
        mesh=grid,
        in_specs=(split, split, split, P(), P(), P(), P(heads, None)),
        out_specs=P(tokens + heads, None),
        check_vma=False,
    )
```

```python
import functools
import math

import jax
import jax.numpy as jnp
from jax import lax
from jax.experimental import pallas as pl
from jax.experimental.pallas import tpu as pltpu
from jax.sharding import Mesh
from jax.sharding import PartitionSpec as P


HD = 128
GROUP = 4
NY, NZ, NX, NC = 4, 16, 4, 2
ROWS = 256
ROW_KEYS = NZ * ROWS
LOW = -1e30
MASKED = -3e30
SCALE = 1.0 / math.sqrt(HD)
EXP2_SCALE = SCALE * math.log2(math.e)
STAT_ROWS = 16
CHUNK = 64
PACK = GROUP * HD + STAT_ROWS
NT = (((1,), (1,)), ((), ()))


def pack_kernel(k_ref, v_ref, out_ref):
    out_ref[:, :HD] = k_ref[...]
    for half in range(2):
        rows = slice(half * HD, (half + 1) * HD)
        out_ref[rows, HD:] = v_ref[rows, :].astype(jnp.float32).T.astype(jnp.bfloat16)


def order_kernel(q_ref, out_ref):
    for x in range(NX):
        for c in range(NC):
            to, at = c * 128 + x * 32, (x * NC + c) * 32
            out_ref[to : to + 32, :] = q_ref[at : at + 32, :]


def query_offsets(shape):
    col = lax.broadcasted_iota(jnp.int32, shape, 1)
    return ((col % 128) // 32 * NC + col // 128) * 32 + col % 32


def fold(q_ref, slot, keys, values, mask, valid, acc, top, total, s_ref):
    def score(h):
        q = q_ref[slot, :, h * HD : (h + 1) * HD]
        new = top[slot, h]
        for n, k in enumerate(keys):
            s = lax.dot_general(k, q, NT, preferred_element_type=jnp.float32)
            if mask is not None:
                s = jnp.where(mask, s, MASKED)
            s_ref[h % 2, n] = s
            peak = jnp.max(s.reshape(ROWS // 8, 8, ROWS), axis=0)
            peak = jnp.max(peak, axis=0, keepdims=True)
            if valid is not None:
                peak = jnp.where(valid[n], peak, LOW)
            new = jnp.maximum(new, peak)
        return new

    new = score(0)
    for h in range(GROUP):
        if h + 1 < GROUP:
            new_next = score(h + 1)
        old = top[slot, h]
        factor = jnp.exp2((old - new) * EXP2_SCALE)
        part = total[slot, h] * factor
        weights = []
        for n in range(len(keys)):
            shift = new[:1] * EXP2_SCALE
            if valid is not None:
                shift = jnp.where(valid[n], shift, -MASKED)
            for r in range(0, ROWS, CHUNK):
                w = jnp.exp2(s_ref[h % 2, n, r : r + CHUNK] * EXP2_SCALE - shift)
                part = part + jnp.sum(w.reshape(CHUNK // 8, 8, ROWS), axis=0)
                weights.append(w.astype(jnp.bfloat16))
        out = jnp.dot(
            jnp.concatenate(values, axis=1),
            jnp.concatenate(weights, axis=0),
            preferred_element_type=jnp.float32,
        )
        top[slot, h] = new
        total[slot, h] = part
        acc[slot, h] = acc[slot, h] * factor[:1] + out
        if h + 1 < GROUP:
            new = new_next


def split_block(block_ref, k_ref, v_ref):
    k_ref[...] = block_ref[:, :HD]
    v_ref[:, :HD] = block_ref[:HD, HD:]
    v_ref[:, HD:] = block_ref[HD:, HD:]


def fold_masked(info, q_ref, slot, k_ref, v_ref, key_start, acc, top, total, s_ref):
    kind, sink, window = info[2], info[3], info[4]
    query_start = (info[0] + slot) * ROW_KEYS + info[1] * ROWS
    needed = (key_start <= query_start + ROWS - 1) & (
        (kind == 1) | (key_start + ROWS - 1 > query_start - window) | (key_start < sink)
    )

    @pl.when(needed)
    def _():
        i = query_start + query_offsets((ROWS, ROWS))
        j = key_start + lax.broadcasted_iota(jnp.int32, (ROWS, ROWS), 0)
        mask = (j <= i) & ((kind == 1) | (j > i - window) | (j < sink))
        fold(q_ref, slot, [k_ref[...]], [v_ref[...]], mask, None, acc, top, total, s_ref)


def first_kernel(kinds, sinks, windows, q_ref, own_ref, acc, top, total, k_ref, v_ref, s_ref):
    info = read_info((kinds, sinks, windows))
    acc[...] = jnp.zeros_like(acc)
    top[...] = jnp.full_like(top, LOW)
    total[...] = jnp.zeros_like(total)
    own_start = info[0] * ROW_KEYS + info[1] * ROWS
    split_block(own_ref, k_ref, v_ref)
    fold_masked(info, q_ref, 0, k_ref, v_ref, own_start, acc, top, total, s_ref)


def stack_kernel(q0_ref, q1_ref, q2_ref, q3_ref, out_ref):
    for slot, ref in enumerate((q0_ref, q1_ref, q2_ref, q3_ref)):
        out_ref[slot] = ref[...]


def step_kernel(
    distances, last, kinds, sinks, windows, q_ref, a_ref, b_ref,
    acc_in, top_in, total_in, acc, top, total, k_ref, v_ref, s_ref
):
    del acc_in, top_in, total_in
    info = read_info((kinds, sinks, windows))
    y, z, kind = info[0], info[1], info[2]
    slots = NY - y
    places = []
    for i, distance in enumerate(distances):
        rows = pl.ds(i * ROWS, ROWS)
        split_block(a_ref.at[rows], k_ref.at[2 * i], v_ref.at[2 * i])
        split_block(b_ref.at[rows], k_ref.at[2 * i + 1], v_ref.at[2 * i + 1])
        places.append(lax.rem(z - distance + NZ, NZ))
        places.append(lax.rem(z + (0 if last else distance), NZ))
    before = [place < z for place in places]

    @pl.when(kind == 1)
    def _():
        any_before = functools.reduce(jnp.logical_or, before)

        @pl.loop(jnp.where(any_before, 0, 1), slots)
        def _(slot):
            for i in range(0, len(places), 2):
                sides = (i, i + 1)
                valid = [(slot > 0) | before[n] for n in sides]
                keys, values = [k_ref[n] for n in sides], [v_ref[n] for n in sides]
                fold(q_ref, slot, keys, values, None, valid, acc, top, total, s_ref)

    @pl.when(kind != 1)
    def _():
        blocks = len(places)

        @pl.loop(0, blocks * slots)
        def _(n):
            slot = n // blocks
            side = n % blocks
            place = places[0]
            for i in range(1, blocks):
                place = jnp.where(side == i, places[i], place)
            skip = (slot == 0) & (place == z)

            @pl.when(jnp.logical_not(skip))
            def _():
                key_start = y * ROW_KEYS + place * ROWS
                fold_masked(
                    info, q_ref, slot, k_ref.at[side], v_ref.at[side], key_start, acc, top, total, s_ref
                )


def finish_kernel(acc, top, total, out_ref):
    y = lax.axis_index("y")
    for target in range(NY):
        slot = jnp.maximum(target - y, 0)
        valid = target >= y
        parts = []
        for h in range(GROUP):
            s = jnp.sum(total[slot, h], axis=0, keepdims=True)
            have = (s > 0.0) & valid
            safe = jnp.where(have, s, 1.0)
            o = jnp.where(have, acc[slot, h] * (1.0 / safe), 0.0).astype(jnp.bfloat16)
            lse = jnp.where(have, top[slot, h][:1] * SCALE + jnp.log(safe), LOW)
            for c in range(NC):
                out_ref[target * NC + c, h * HD : (h + 1) * HD, :] = o[:, c * 128 : (c + 1) * 128]
            high = lse.astype(jnp.bfloat16).astype(jnp.float32)
            rest = lse - high
            mid = rest.astype(jnp.bfloat16).astype(jnp.float32)
            parts += [high, mid, rest - mid]
        parts += [jnp.zeros_like(parts[0])] * (STAT_ROWS - len(parts))
        packed = jnp.concatenate(parts, axis=0).astype(jnp.bfloat16)
        for c in range(NC):
            out_ref[target * NC + c, GROUP * HD :, :] = packed[:, c * 128 : (c + 1) * 128]


def project_kernel(parts_ref, own_w_ref, other_w_ref, out_ref, mix):
    @pl.when(pl.program_id(0) == 0)
    def _():
        core = lax.axis_index("core")
        for side in range(NC):
            source = core if side == 0 else 1 - core
            stats = [
                parts_ref[y * NC + source, GROUP * HD :, :].astype(jnp.float32) for y in range(NY)
            ]
            for h in range(GROUP):
                lse = [s[3 * h : 3 * h + 1] + s[3 * h + 1 : 3 * h + 2] + s[3 * h + 2 : 3 * h + 3] for s in stats]
                peak = functools.reduce(jnp.maximum, lse)
                weight = [jnp.exp(v - peak) for v in lse]
                norm = 1.0 / functools.reduce(jnp.add, weight)
                out = None
                for y in range(NY):
                    o = parts_ref[y * NC + source, h * HD : (h + 1) * HD, :].astype(jnp.float32)
                    o = o * (weight[y] * norm)
                    out = o if out is None else out + o
                mix[side, :, h * HD : (h + 1) * HD] = out.T.astype(jnp.bfloat16)

    out_ref[...] = (
        jnp.dot(mix[0], own_w_ref[...], preferred_element_type=jnp.float32)
        + jnp.dot(mix[1], other_w_ref[...], preferred_element_type=jnp.float32)
    ).astype(jnp.bfloat16)


def read_info(heads):
    y, z = lax.axis_index("y"), lax.axis_index("z")
    core = lax.axis_index("core")
    head = lax.axis_index("x") * NC + core
    return (y, z, *(table[head] for table in heads), core)


VMEM_SPEC = pl.BlockSpec(memory_space=pltpu.VMEM)
SMEM_SPEC = pl.BlockSpec(memory_space=pltpu.SMEM)
STATE = [
    jax.ShapeDtypeStruct((NY, GROUP, HD, ROWS), jnp.float32),
    jax.ShapeDtypeStruct((NY, GROUP, 8, ROWS), jnp.float32),
    jax.ShapeDtypeStruct((NY, GROUP, 8, ROWS), jnp.float32),
]


def params(mib=24):
    return pltpu.CompilerParams(vmem_limit_bytes=mib << 20)


ROUNDS = {1: (1, (1,)), 2: (2, (2, 3)), 3: (2, (4, 5)), 4: (2, (6, 7)), 5: (1, (8,))}


def body(queries, keys, values, head_kind, sink_len, window_len, w_out):
    heads = (head_kind, sink_len, window_len)
    own = pl.pallas_call(
        pack_kernel,
        grid=(1,),
        out_shape=jax.ShapeDtypeStruct((ROWS, 2 * HD), jnp.bfloat16),
        in_specs=[pl.BlockSpec((ROWS, HD), lambda i: (0, 0))] * 2,
        out_specs=VMEM_SPEC,
        compiler_params=params(),
        name="pack",
    )(keys, values)
    queries = pl.pallas_call(
        order_kernel,
        out_shape=jax.ShapeDtypeStruct(queries.shape, jnp.bfloat16),
        in_specs=[VMEM_SPEC],
        out_specs=VMEM_SPEC,
        compiler_params=params(),
        name="order",
    )(queries)

    a, b = {0: own}, {0: own}
    cost = pl.CostEstimate(flops=1 << 30, bytes_accessed=8 << 20, transcendentals=1 << 22)
    state = pl.pallas_call(
        first_kernel,
        out_shape=STATE,
        in_specs=[SMEM_SPEC] * 3 + [VMEM_SPEC] * 2,
        out_specs=[VMEM_SPEC] * 3,
        scratch_shapes=[
            pltpu.VMEM((ROWS, HD), jnp.bfloat16),
            pltpu.VMEM((HD, ROWS), jnp.bfloat16),
            pltpu.VMEM((2, 2, ROWS, ROWS), jnp.float32),
        ],
        compiler_params=params(),
        cost_estimate=cost,
        name="first",
    )(*heads, queries[None], own)

    final = len(ROUNDS)
    send_a = send_b = own
    for d, (hops, _) in ROUNDS.items():
        a[d] = lax.ppermute(send_a, "z", [(i, (i + hops) % NZ) for i in range(NZ)])
        send_a = jnp.concatenate([own, a[1]], axis=0) if d == 1 else a[d]
        if d == final:
            b[d] = own
            break
        b[d] = lax.ppermute(send_b, "z", [(i, (i - hops) % NZ) for i in range(NZ)])
        send_b = jnp.concatenate([own, b[1]], axis=0) if d == 1 else b[d]
        if d + 1 == final:
            send_a = a[d][ROWS:]
    received = []
    for k in range(1, NY):
        received.append(lax.ppermute(queries, "y", [(i, i - k) for i in range(k, NY)]))
    other_w = lax.ppermute(w_out, "core", [(0, 1), (1, 0)])

    slots = pl.pallas_call(
        stack_kernel,
        out_shape=jax.ShapeDtypeStruct((NY, ROWS, GROUP * HD), jnp.bfloat16),
        in_specs=[VMEM_SPEC] * NY,
        out_specs=VMEM_SPEC,
        compiler_params=params(),
        name="stack",
    )(queries, *received)
    for d, (_, distances) in ROUNDS.items():
        state = pl.pallas_call(
            functools.partial(step_kernel, distances, d == final),
            out_shape=STATE,
            in_specs=[SMEM_SPEC] * 3 + [VMEM_SPEC] * 6,
            out_specs=[VMEM_SPEC] * 3,
            scratch_shapes=[
                pltpu.VMEM((2 * len(distances), ROWS, HD), jnp.bfloat16),
                pltpu.VMEM((2 * len(distances), HD, ROWS), jnp.bfloat16),
                pltpu.VMEM((2, 2, ROWS, ROWS), jnp.float32),
            ],
            input_output_aliases={6: 0, 7: 1, 8: 2},
            compiler_params=params(),
            cost_estimate=cost,
            name="step",
        )(*heads, slots, a[d], b[d], *state)

    packed = pl.pallas_call(
        finish_kernel,
        out_shape=jax.ShapeDtypeStruct((NY * NC, PACK, ROWS // NC), jnp.bfloat16),
        in_specs=[VMEM_SPEC] * 3,
        out_specs=VMEM_SPEC,
        compiler_params=params(),
        name="finish",
    )(*state)
    parts = lax.all_to_all(packed, ("y", "core"), 0, 0, tiled=True)

    width = 1024
    mixed = pl.pallas_call(
        project_kernel,
        out_shape=jax.ShapeDtypeStruct((ROWS // NC, w_out.shape[1]), jnp.bfloat16),
        grid=(w_out.shape[1] // width,),
        in_specs=[
            VMEM_SPEC,
            pl.BlockSpec((GROUP * HD, width), lambda i: (0, i)),
            pl.BlockSpec((GROUP * HD, width), lambda i: (0, i)),
        ],
        out_specs=pl.BlockSpec((ROWS // NC, width), lambda i: (0, i)),
        scratch_shapes=[pltpu.VMEM((NC, ROWS // NC, GROUP * HD), jnp.bfloat16)],
        compiler_params=params(),
        name="project",
    )(parts, w_out, other_w)
    pieces = lax.all_to_all(mixed.reshape(NX, 32, -1), "x", 0, 0, tiled=True)
    return jnp.sum(pieces.astype(jnp.float32), axis=0).astype(jnp.bfloat16)


def solution(mesh):
    grid = Mesh(mesh.devices.reshape(NY, NZ, NX, NC), ("y", "z", "x", "core"))
    tokens, heads = ("y", "z"), ("x", "core")
    split = P(tokens, heads)

    return jax.shard_map(
        body,
        mesh=grid,
        in_specs=(split, split, split, P(), P(), P(), P(heads, None)),
        out_specs=P(tokens + heads, None),
        check_vma=False,
    )
```

```python
import functools
import math

import jax
import jax.numpy as jnp
from jax import lax
from jax.experimental import pallas as pl
from jax.experimental.pallas import tpu as pltpu
from jax.sharding import Mesh
from jax.sharding import PartitionSpec as P


HD = 128
GROUP = 4
NY, NZ, NX, NC = 4, 16, 4, 2
ROWS = 256
ROW_KEYS = NZ * ROWS
LOW = -1e30
MASKED = -3e30
SCALE = 1.0 / math.sqrt(HD)
EXP2_SCALE = SCALE * math.log2(math.e)
STAT_ROWS = 16
CHUNK = 64
PACK = GROUP * HD + STAT_ROWS
NT = (((1,), (1,)), ((), ()))


def pack_kernel(k_ref, v_ref, out_ref):
    out_ref[:, :HD] = k_ref[...]
    for half in range(2):
        rows = slice(half * HD, (half + 1) * HD)
        out_ref[rows, HD:] = v_ref[rows, :].astype(jnp.float32).T.astype(jnp.bfloat16)


def order_kernel(q_ref, out_ref):
    for x in range(NX):
        for c in range(NC):
            to, at = c * 128 + x * 32, (x * NC + c) * 32
            out_ref[to : to + 32, :] = q_ref[at : at + 32, :]


def query_offsets(shape):
    col = lax.broadcasted_iota(jnp.int32, shape, 1)
    return ((col % 128) // 32 * NC + col // 128) * 32 + col % 32


def fold(q_ref, slot, keys, values, mask, valid, acc, top, total, s_ref):
    def score(h):
        q = q_ref[slot, :, h * HD : (h + 1) * HD]
        new = top[slot, h]
        for n, k in enumerate(keys):
            s = lax.dot_general(k, q, NT, preferred_element_type=jnp.float32)
            if mask is not None:
                s = jnp.where(mask, s, MASKED)
            s_ref[h % 2, n] = s
            peak = jnp.max(s.reshape(ROWS // 8, 8, ROWS), axis=0)
            peak = jnp.max(peak, axis=0, keepdims=True)
            if valid is not None:
                peak = jnp.where(valid[n], peak, LOW)
            new = jnp.maximum(new, peak)
        return new

    new = score(0)
    for h in range(GROUP):
        if h + 1 < GROUP:
            new_next = score(h + 1)
        old = top[slot, h]
        factor = jnp.exp2((old - new) * EXP2_SCALE)
        part = total[slot, h] * factor
        weights = []
        for n in range(len(keys)):
            shift = new[:1] * EXP2_SCALE
            if valid is not None:
                shift = jnp.where(valid[n], shift, -MASKED)
            for r in range(0, ROWS, CHUNK):
                w = jnp.exp2(s_ref[h % 2, n, r : r + CHUNK] * EXP2_SCALE - shift)
                part = part + jnp.sum(w.reshape(CHUNK // 8, 8, ROWS), axis=0)
                weights.append(w.astype(jnp.bfloat16))
        out = jnp.dot(
            jnp.concatenate(values, axis=1),
            jnp.concatenate(weights, axis=0),
            preferred_element_type=jnp.float32,
        )
        top[slot, h] = new
        total[slot, h] = part
        acc[slot, h] = acc[slot, h] * factor[:1] + out
        if h + 1 < GROUP:
            new = new_next


def split_block(block_ref, k_ref, v_ref):
    k_ref[...] = block_ref[:, :HD]
    v_ref[:, :HD] = block_ref[:HD, HD:]
    v_ref[:, HD:] = block_ref[HD:, HD:]


def fold_masked(info, q_ref, slot, k_ref, v_ref, key_start, acc, top, total, s_ref):
    kind, sink, window = info[2], info[3], info[4]
    query_start = (info[0] + slot) * ROW_KEYS + info[1] * ROWS
    needed = (key_start <= query_start + ROWS - 1) & (
        (kind == 1) | (key_start + ROWS - 1 > query_start - window) | (key_start < sink)
    )

    @pl.when(needed)
    def _():
        i = query_start + query_offsets((ROWS, ROWS))
        j = key_start + lax.broadcasted_iota(jnp.int32, (ROWS, ROWS), 0)
        mask = (j <= i) & ((kind == 1) | (j > i - window) | (j < sink))
        fold(q_ref, slot, [k_ref[...]], [v_ref[...]], mask, None, acc, top, total, s_ref)


def first_kernel(kinds, sinks, windows, q_ref, own_ref, acc, top, total, k_ref, v_ref, s_ref):
    info = read_info((kinds, sinks, windows))
    acc[...] = jnp.zeros_like(acc)
    top[...] = jnp.full_like(top, LOW)
    total[...] = jnp.zeros_like(total)
    own_start = info[0] * ROW_KEYS + info[1] * ROWS
    split_block(own_ref, k_ref, v_ref)
    fold_masked(info, q_ref, 0, k_ref, v_ref, own_start, acc, top, total, s_ref)


def stack_kernel(q0_ref, q1_ref, q2_ref, q3_ref, out_ref):
    for slot, ref in enumerate((q0_ref, q1_ref, q2_ref, q3_ref)):
        out_ref[slot] = ref[...]


def step_kernel(
    distances, last, kinds, sinks, windows, q_ref, a_ref, b_ref,
    acc_in, top_in, total_in, acc, top, total, k_ref, v_ref, s_ref
):
    del acc_in, top_in, total_in
    info = read_info((kinds, sinks, windows))
    y, z, kind = info[0], info[1], info[2]
    slots = NY - y
    places = []
    for i, distance in enumerate(distances):
        rows = pl.ds(i * ROWS, ROWS)
        split_block(a_ref.at[rows], k_ref.at[2 * i], v_ref.at[2 * i])
        split_block(b_ref.at[rows], k_ref.at[2 * i + 1], v_ref.at[2 * i + 1])
        places.append(lax.rem(z - distance + NZ, NZ))
        places.append(lax.rem(z + (0 if last else distance), NZ))
    before = [place < z for place in places]

    @pl.when(kind == 1)
    def _():
        any_before = functools.reduce(jnp.logical_or, before)

        @pl.loop(jnp.where(any_before, 0, 1), slots)
        def _(slot):
            sides = range(len(places))
            valid = [(slot > 0) | before[n] for n in sides]
            keys, values = [k_ref[n] for n in sides], [v_ref[n] for n in sides]
            fold(q_ref, slot, keys, values, None, valid, acc, top, total, s_ref)

    @pl.when(kind != 1)
    def _():
        blocks = len(places)

        @pl.loop(0, blocks * slots)
        def _(n):
            slot = n // blocks
            side = n % blocks
            place = places[0]
            for i in range(1, blocks):
                place = jnp.where(side == i, places[i], place)
            skip = (slot == 0) & (place == z)

            @pl.when(jnp.logical_not(skip))
            def _():
                key_start = y * ROW_KEYS + place * ROWS
                fold_masked(
                    info, q_ref, slot, k_ref.at[side], v_ref.at[side], key_start, acc, top, total, s_ref
                )


def finish_kernel(acc, top, total, out_ref):
    y = lax.axis_index("y")
    for target in range(NY):
        slot = jnp.maximum(target - y, 0)
        valid = target >= y
        parts = []
        for h in range(GROUP):
            s = jnp.sum(total[slot, h], axis=0, keepdims=True)
            have = (s > 0.0) & valid
            safe = jnp.where(have, s, 1.0)
            o = jnp.where(have, acc[slot, h] * (1.0 / safe), 0.0).astype(jnp.bfloat16)
            lse = jnp.where(have, top[slot, h][:1] * SCALE + jnp.log(safe), LOW)
            for c in range(NC):
                out_ref[target * NC + c, h * HD : (h + 1) * HD, :] = o[:, c * 128 : (c + 1) * 128]
            high = lse.astype(jnp.bfloat16).astype(jnp.float32)
            rest = lse - high
            mid = rest.astype(jnp.bfloat16).astype(jnp.float32)
            parts += [high, mid, rest - mid]
        parts += [jnp.zeros_like(parts[0])] * (STAT_ROWS - len(parts))
        packed = jnp.concatenate(parts, axis=0).astype(jnp.bfloat16)
        for c in range(NC):
            out_ref[target * NC + c, GROUP * HD :, :] = packed[:, c * 128 : (c + 1) * 128]


def project_kernel(parts_ref, own_w_ref, other_w_ref, out_ref, mix):
    @pl.when(pl.program_id(0) == 0)
    def _():
        core = lax.axis_index("core")
        for side in range(NC):
            source = core if side == 0 else 1 - core
            stats = [
                parts_ref[y * NC + source, GROUP * HD :, :].astype(jnp.float32) for y in range(NY)
            ]
            for h in range(GROUP):
                lse = [s[3 * h : 3 * h + 1] + s[3 * h + 1 : 3 * h + 2] + s[3 * h + 2 : 3 * h + 3] for s in stats]
                peak = functools.reduce(jnp.maximum, lse)
                weight = [jnp.exp(v - peak) for v in lse]
                norm = 1.0 / functools.reduce(jnp.add, weight)
                out = None
                for y in range(NY):
                    o = parts_ref[y * NC + source, h * HD : (h + 1) * HD, :].astype(jnp.float32)
                    o = o * (weight[y] * norm)
                    out = o if out is None else out + o
                mix[side, :, h * HD : (h + 1) * HD] = out.T.astype(jnp.bfloat16)

    out_ref[...] = (
        jnp.dot(mix[0], own_w_ref[...], preferred_element_type=jnp.float32)
        + jnp.dot(mix[1], other_w_ref[...], preferred_element_type=jnp.float32)
    ).astype(jnp.bfloat16)


def read_info(heads):
    y, z = lax.axis_index("y"), lax.axis_index("z")
    core = lax.axis_index("core")
    head = lax.axis_index("x") * NC + core
    return (y, z, *(table[head] for table in heads), core)


VMEM_SPEC = pl.BlockSpec(memory_space=pltpu.VMEM)
SMEM_SPEC = pl.BlockSpec(memory_space=pltpu.SMEM)
STATE = [
    jax.ShapeDtypeStruct((NY, GROUP, HD, ROWS), jnp.float32),
    jax.ShapeDtypeStruct((NY, GROUP, 8, ROWS), jnp.float32),
    jax.ShapeDtypeStruct((NY, GROUP, 8, ROWS), jnp.float32),
]


def params(mib=24):
    return pltpu.CompilerParams(vmem_limit_bytes=mib << 20)


ROUNDS = {1: (1, (1,)), 2: (2, (2, 3)), 3: (2, (4, 5)), 4: (2, (6, 7)), 5: (1, (8,))}
FOLDS = (2, 1, 3, 4, 5)


def body(queries, keys, values, head_kind, sink_len, window_len, w_out):
    heads = (head_kind, sink_len, window_len)
    own = pl.pallas_call(
        pack_kernel,
        grid=(1,),
        out_shape=jax.ShapeDtypeStruct((ROWS, 2 * HD), jnp.bfloat16),
        in_specs=[pl.BlockSpec((ROWS, HD), lambda i: (0, 0))] * 2,
        out_specs=VMEM_SPEC,
        compiler_params=params(),
        name="pack",
    )(keys, values)
    queries = pl.pallas_call(
        order_kernel,
        out_shape=jax.ShapeDtypeStruct(queries.shape, jnp.bfloat16),
        in_specs=[VMEM_SPEC],
        out_specs=VMEM_SPEC,
        compiler_params=params(),
        name="order",
    )(queries)

    a, b = {0: own}, {0: own}
    cost = pl.CostEstimate(flops=1 << 30, bytes_accessed=8 << 20, transcendentals=1 << 22)
    state = pl.pallas_call(
        first_kernel,
        out_shape=STATE,
        in_specs=[SMEM_SPEC] * 3 + [VMEM_SPEC] * 2,
        out_specs=[VMEM_SPEC] * 3,
        scratch_shapes=[
            pltpu.VMEM((ROWS, HD), jnp.bfloat16),
            pltpu.VMEM((HD, ROWS), jnp.bfloat16),
            pltpu.VMEM((2, 2, ROWS, ROWS), jnp.float32),
        ],
        compiler_params=params(),
        cost_estimate=cost,
        name="first",
    )(*heads, queries[None], own)

    final = len(ROUNDS)
    send_a = send_b = own
    for d, (hops, _) in ROUNDS.items():
        a[d] = lax.ppermute(send_a, "z", [(i, (i + hops) % NZ) for i in range(NZ)])
        send_a = jnp.concatenate([own, a[1]], axis=0) if d == 1 else a[d]
        if d == final:
            b[d] = own
            break
        b[d] = lax.ppermute(send_b, "z", [(i, (i - hops) % NZ) for i in range(NZ)])
        send_b = jnp.concatenate([own, b[1]], axis=0) if d == 1 else b[d]
        if d + 1 == final:
            send_a = a[d][ROWS:]
    received = []
    for k in range(1, NY):
        received.append(lax.ppermute(queries, "y", [(i, i - k) for i in range(k, NY)]))
    other_w = lax.ppermute(w_out, "core", [(0, 1), (1, 0)])

    slots = pl.pallas_call(
        stack_kernel,
        out_shape=jax.ShapeDtypeStruct((NY, ROWS, GROUP * HD), jnp.bfloat16),
        in_specs=[VMEM_SPEC] * NY,
        out_specs=VMEM_SPEC,
        compiler_params=params(),
        name="stack",
    )(queries, *received)
    for d in FOLDS:
        distances = ROUNDS[d][1]
        state = pl.pallas_call(
            functools.partial(step_kernel, distances, d == final),
            out_shape=STATE,
            in_specs=[SMEM_SPEC] * 3 + [VMEM_SPEC] * 6,
            out_specs=[VMEM_SPEC] * 3,
            scratch_shapes=[
                pltpu.VMEM((2 * len(distances), ROWS, HD), jnp.bfloat16),
                pltpu.VMEM((2 * len(distances), HD, ROWS), jnp.bfloat16),
                pltpu.VMEM((2, 2 * len(distances), ROWS, ROWS), jnp.float32),
            ],
            input_output_aliases={6: 0, 7: 1, 8: 2},
            compiler_params=params(),
            cost_estimate=cost,
            name="step",
        )(*heads, slots, a[d], b[d], *state)

    packed = pl.pallas_call(
        finish_kernel,
        out_shape=jax.ShapeDtypeStruct((NY * NC, PACK, ROWS // NC), jnp.bfloat16),
        in_specs=[VMEM_SPEC] * 3,
        out_specs=VMEM_SPEC,
        compiler_params=params(),
        name="finish",
    )(*state)
    parts = lax.all_to_all(packed, ("y", "core"), 0, 0, tiled=True)

    width = 1024
    mixed = pl.pallas_call(
        project_kernel,
        out_shape=jax.ShapeDtypeStruct((ROWS // NC, w_out.shape[1]), jnp.bfloat16),
        grid=(w_out.shape[1] // width,),
        in_specs=[
            VMEM_SPEC,
            pl.BlockSpec((GROUP * HD, width), lambda i: (0, i)),
            pl.BlockSpec((GROUP * HD, width), lambda i: (0, i)),
        ],
        out_specs=pl.BlockSpec((ROWS // NC, width), lambda i: (0, i)),
        scratch_shapes=[pltpu.VMEM((NC, ROWS // NC, GROUP * HD), jnp.bfloat16)],
        compiler_params=params(),
        name="project",
    )(parts, w_out, other_w)
    pieces = lax.all_to_all(mixed.reshape(NX, 32, -1), "x", 0, 0, tiled=True)
    return jnp.sum(pieces.astype(jnp.float32), axis=0).astype(jnp.bfloat16)


def solution(mesh):
    grid = Mesh(mesh.devices.reshape(NY, NZ, NX, NC), ("y", "z", "x", "core"))
    tokens, heads = ("y", "z"), ("x", "core")
    split = P(tokens, heads)

    return jax.shard_map(
        body,
        mesh=grid,
        in_specs=(split, split, split, P(), P(), P(), P(heads, None)),
        out_specs=P(tokens + heads, None),
        check_vma=False,
    )
```
